32 devices in a mesh: groups: 2 (over x), frames: 16 (over z, y, core).
Axes of the slice: x: 2, y: 2, z: 4, core: 2. Of those that a mesh axis runs over, the one named last changes fastest.
Arguments:
- video: float32 [4, 16, 256, 256], P('groups', 'frames'), parts along dimension 0, may hold values from -9 to 9
- clip_start: int32 [4], P('groups'), parts along dimension 0, may hold values from 0 to 7
- gain_space: float32 [256], replicated, may hold values from 0.1 to 1.9
- qkv_space: float32 [256, 768], replicated, may hold values from -0.375 to 0.375
- out_space: float32 [256, 256], replicated, may hold values from -0.375 to 0.375
- gain_time: float32 [256], replicated, may hold values from 0.1 to 1.9
- qkv_time: float32 [256, 768], replicated, may hold values from -0.375 to 0.375
- out_time: float32 [256, 256], replicated, may hold values from -0.375 to 0.375
- code_sums: float32 [8192, 256], P(('groups', 'frames')), parts along dimension 0, may hold values from -12 to 12
- code_counts: float32 [8192], P(('groups', 'frames')), parts along dimension 0, may hold values from 1 to 10
Outputs:
- latents: float32 [4, 16, 256, 256], P('groups', None, 'frames'), parts along dimension 0
- new_sums: float32 [8192, 256], P(('groups', 'frames')), parts along dimension 0
- new_counts: float32 [8192], P(('groups', 'frames')), parts along dimension 0
- new_codebook: float32 [8192, 256], P(('groups', 'frames')), parts along dimension 0
The draws below stay inside these ranges and needn't reach their ends.
There are 2 independent parts, one for each index of `groups`. The reference program is written for one: setup_inputs(seed, part) draws one part's arguments, and reference() takes and returns one part's arrays. A program takes and returns all parts, laid end to end along the dimension named above; an argument that names none is the same for every part. Nothing has to cross between parts.
All inputs are finite; a program needn't handle non-finite values.
Results may differ from the reference program's by a relative error of at most 0.0003.
Values sent between devices are 32-bit elements; how exact they have to be, the bound alone decides.
A program may use at most 64 MiB of HBM per device.

```python
import math
import jax
import jax.numpy as jnp
from jax import lax

D = 256
HEADS = 4
HW = 256
K = 4096
CLIPS = 2
FRAMES = 16


def centre_count():
    return max(K // 16, 2)


def centre_rows(key):
    return jax.random.truncated_normal(jax.random.fold_in(key, 7001), -4.0, 4.0, (centre_count(), D), jnp.float32)


def draw_video(key, part):
    centres = centre_rows(key)
    shape_tok = (CLIPS, FRAMES, HW)
    first_pick = jax.random.randint(jax.random.fold_in(key, 7002), shape_tok, 0, centre_count())
    second_pick = jax.random.randint(jax.random.fold_in(key, 7003), shape_tok, 0, centre_count())
    chosen = jnp.minimum(first_pick, second_pick)
    picked = jnp.take(centres, chosen, axis=0)
    amplitude = 1.2
    noise = 0.9 * jax.random.truncated_normal(jax.random.fold_in(key, 7004), -4.0, 4.0, shape_tok + (D,), jnp.float32)
    return (amplitude * picked + noise).astype(jnp.float32)


def draw_code_sums(key, part):
    centres = centre_rows(key)
    owner = jax.random.permutation(jax.random.fold_in(key, 7006), jnp.arange(K, dtype=jnp.int32)) % centre_count()
    picked = jnp.take(centres, owner, axis=0)
    row_scale = jax.random.uniform(jax.random.fold_in(key, 7007), (K, 1), jnp.float32, 0.5, 1.5)
    noise = 0.8 * jax.random.truncated_normal(jax.random.fold_in(key, 7008), -4.0, 4.0, (K, D), jnp.float32)
    return (row_scale * (picked + noise)).astype(jnp.float32)


def block_scale(key, shape, pieces, low, top_value):
    def one(dim, parts):
        draws = jax.random.uniform(jax.random.fold_in(jax.random.fold_in(key, 6), dim), (parts,), jnp.float32, low / len(pieces), top_value / len(pieces))
        return jnp.repeat(jnp.exp(draws), shape[dim] // parts).reshape((-1,) + (1,) * (len(shape) - dim - 1))

    loudness = one(*pieces[0])
    for cut in pieces[1:]:
        loudness = loudness * one(*cut)
    return loudness


def normal_values(rng, shape, scale, reach, held_as=jnp.bfloat16):
    drawn = jax.random.normal(rng, shape, jnp.float32) * scale
    return jnp.minimum(jnp.maximum(drawn, -reach), reach).astype(held_as)


def setup_inputs(seed: int = 0, part: int = 0) -> dict:
    keys = jax.random.split(jax.random.key(seed), 11)
    part_keys = jax.random.split(jax.random.fold_in(keys[10], part), 11)
    return {
        "video": draw_video(jax.random.fold_in(jax.random.fold_in(keys[10], part), 71), part),
        "clip_start": jax.random.randint(part_keys[1], (CLIPS,), 0, FRAMES // 2).astype(jnp.int32),
        "gain_space": jnp.clip(1.0 + 0.18 * jax.random.normal(keys[2], (D,), jnp.float32), 0.1, 1.9),
        "qkv_space": normal_values(keys[3], (D, 3 * D), D ** -0.5, 0.375, jnp.float32),
        "out_space": normal_values(keys[4], (D, D), D ** -0.5, 0.375, jnp.float32),
        "gain_time": jnp.clip(1.0 + 0.18 * jax.random.normal(keys[5], (D,), jnp.float32), 0.1, 1.9),
        "qkv_time": normal_values(keys[6], (D, 3 * D), D ** -0.5, 0.375, jnp.float32),
        "out_time": normal_values(keys[7], (D, D), D ** -0.5, 0.375, jnp.float32),
        "code_sums": draw_code_sums(jax.random.fold_in(jax.random.fold_in(keys[10], part), 71), part),
        "code_counts": jnp.clip(jnp.exp(math.log(10.0) - 2.3025851 * jax.random.uniform(part_keys[9], (K,), jnp.float32) ** block_scale(part_keys[9], (K,), ((0, 16),), -0.2, 0.2)), 1.0, 10.0),
    }


ATTN_SCALE = 10.0
SOFTMAX_WARMTH = 0.05
DECAY_RATE = 0.9
EPSILON = 1e-06
TOP_PRECISION = lax.Precision.HIGHEST

def rms_norm(values, gain_vec):
    return values * lax.rsqrt(lax.optimization_barrier(jnp.mean(values * values, -1, keepdims=True)) + EPSILON) * gain_vec

def unit_vec(values):
    return values * lax.rsqrt(lax.optimization_barrier(jnp.sum(values * values, -1, keepdims=True)) + EPSILON)

def spatial_block(one_frame, gain_vec, w_qkv, w_out):
    width = one_frame.shape[-1]
    normed = rms_norm(one_frame, gain_vec)
    packed = jnp.dot(normed, w_qkv, precision=TOP_PRECISION)
    queries = unit_vec(packed[:, :width].reshape(-1, HEADS, width // HEADS))
    key_vecs = unit_vec(packed[:, width:2 * width].reshape(-1, HEADS, width // HEADS))
    values = packed[:, 2 * width:].reshape(-1, HEADS, width // HEADS)
    scores = ATTN_SCALE * jnp.einsum('qhd,khd->hqk', queries, key_vecs, precision=TOP_PRECISION)
    assignment_weights = jnp.exp(scores)
    totals = lax.optimization_barrier(jnp.sum(assignment_weights, -1)).T[:, :, None]
    mixed = jnp.einsum('hqk,khd->qhd', assignment_weights, values, precision=TOP_PRECISION) / totals
    return one_frame + jnp.dot(mixed.reshape(-1, width), w_out, precision=TOP_PRECISION)

def time_block(spaced, clip_start, gain_vec, w_qkv, w_out):
    clips, frames, places, width = spaced.shape
    normed = rms_norm(spaced, gain_vec)
    packed = jnp.einsum('ctpd,de->ctpe', normed, w_qkv, precision=TOP_PRECISION)
    shape_heads = (clips, frames, places, HEADS, width // HEADS)
    queries = unit_vec(packed[..., :width].reshape(shape_heads))
    key_vecs = unit_vec(packed[..., width:2 * width].reshape(shape_heads))
    values = packed[..., 2 * width:].reshape(shape_heads)
    scores = ATTN_SCALE * jnp.einsum('ctphd,csphd->cphts', queries, key_vecs, precision=TOP_PRECISION)
    later = jnp.arange(frames, dtype=jnp.int32)[:, None]
    earlier = jnp.arange(frames, dtype=jnp.int32)[None, :]
    allowed = (earlier <= later)[None] & ((earlier[None] >= clip_start[:, None, None]) | (earlier == later)[None])
    assignment_weights = jnp.exp(scores) * allowed[:, None, None, :, :].astype(jnp.float32)
    totals = jnp.transpose(lax.optimization_barrier(jnp.sum(assignment_weights, -1)), (0, 3, 1, 2))[..., None]
    mixed = jnp.einsum('cphts,csphd->ctphd', assignment_weights, values, precision=TOP_PRECISION) / totals
    return spaced + jnp.einsum('ctpd,de->ctpe', mixed.reshape(clips, frames, places, width), w_out, precision=TOP_PRECISION)

def reference(video, clip_start, gain_space, qkv_space, out_space, gain_time, qkv_time, out_time, code_sums, code_counts):
    clips, frames, places, width = video.shape
    flat_frames = video.reshape(clips * frames, places, width)
    spaced = lax.map(lambda one_frame: spatial_block(one_frame, gain_space, qkv_space, out_space), flat_frames)
    spaced = spaced.reshape(clips, frames, places, width)
    latents = time_block(spaced, clip_start, gain_time, qkv_time, out_time)
    unit_token_vectors = unit_vec(latents.reshape(clips * frames, places, width))
    unit_code_vectors = unit_vec(code_sums / code_counts[:, None])

    def accumulate(carry, rows_per_block):
        sums_acc, counts_acc = carry
        assignment_weights = jnp.exp(jnp.dot(rows_per_block, unit_code_vectors.T, precision=TOP_PRECISION) / SOFTMAX_WARMTH)
        probs = assignment_weights / lax.optimization_barrier(jnp.sum(assignment_weights, 1, keepdims=True))
        sums_acc = sums_acc + lax.dot_general(probs, rows_per_block, (((0,), (0,)), ((), ())), precision=TOP_PRECISION)
        counts_acc = counts_acc + lax.optimization_barrier(jnp.sum(probs, 0))
        return ((sums_acc, counts_acc), None)
    start_carry = (jnp.zeros(code_sums.shape, jnp.float32), jnp.zeros(code_counts.shape, jnp.float32))
    (term_sums, term_counts), _ = lax.scan(accumulate, start_carry, unit_token_vectors)
    new_sums = DECAY_RATE * code_sums + (1.0 - DECAY_RATE) * term_sums
    new_counts = DECAY_RATE * code_counts + (1.0 - DECAY_RATE) * term_counts
    new_codebook = new_sums / new_counts[:, None]
    return (latents, new_sums, new_counts, new_codebook)
```

```python
import functools

import jax
import jax.numpy as jnp
from jax import lax
from jax.experimental import pallas as pl
from jax.experimental.pallas import tpu as pltpu
from jax.sharding import PartitionSpec as P

HEADS = 4
ATTN_SCALE = 10.0
SOFTMAX_WARMTH = 0.05
DECAY_RATE = 0.9
EPSILON = 1e-06
F32 = jnp.float32
BF16 = jnp.bfloat16
NN = (((1,), (0,)), ((), ()))
NT = (((1,), (1,)), ((), ()))


def split(a):
    hi = a.astype(BF16)
    return hi, (a - hi.astype(F32)).astype(BF16)


def dot(a, b, dims=NN):
    return lax.dot_general(a, b, dims, preferred_element_type=F32)


def dot3(a, b, dims=NN):
    return dot(a[0], b[0], dims) + (dot(a[0], b[1], dims) + dot(a[1], b[0], dims))


def dot2(a, b, dims=NN):
    return dot(a[0], b, dims) + dot(a[1], b, dims)


def attention(x, gain, w_qkv, w_out, mask):
    rows, width = x.shape
    hd = width // HEADS
    pair = 2 * hd
    lane_i = lax.broadcasted_iota(jnp.int32, (width, width), 0) // hd
    lane_j = lax.broadcasted_iota(jnp.int32, (width, width), 1) // hd
    same_head = jnp.where(lane_i == lane_j, 1.0, 0.0).astype(BF16)
    first = lax.broadcasted_iota(jnp.int32, (rows, pair), 1) < hd

    def product(a, w):
        ah, al = split(a)
        both = dot(jnp.concatenate([ah, al], 0), w[0])
        return both[:rows] + (both[rows:] + dot(ah, w[1]))

    normed = x * lax.rsqrt(jnp.mean(x * x, -1, keepdims=True) + EPSILON) * gain
    packed = product(normed, w_qkv)
    q, k, v = packed[:, :width], packed[:, width : 2 * width], packed[:, 2 * width :]
    squares = dot(jnp.concatenate(split(q * q) + split(k * k), 0), same_head)
    q = q * lax.rsqrt(squares[:rows] + squares[rows : 2 * rows] + EPSILON) * ATTN_SCALE
    k = k * lax.rsqrt(squares[2 * rows : 3 * rows] + squares[3 * rows :] + EPSILON)
    mixed = []
    for p in range(HEADS // 2):
        at = slice(p * pair, (p + 1) * pair)
        qh = q[:, at].astype(BF16).astype(F32)
        kh = k[:, at].astype(BF16).astype(F32)
        ql = pltpu.roll(q[:, at] - qh, hd, 1)
        kr = pltpu.roll(kh, hd, 1)
        kl = k[:, at] - kh
        s_a = dot(
            jnp.concatenate([jnp.where(first, qh, ql), jnp.where(first, qh, 0.0)], 1).astype(BF16),
            jnp.concatenate([jnp.where(first, kh, kr), kl], 1).astype(BF16), NT,
        )
        s_b = dot(
            jnp.concatenate([jnp.where(first, ql, qh), jnp.where(first, 0.0, qh)], 1).astype(BF16),
            jnp.concatenate([jnp.where(first, kr, kh), kl], 1).astype(BF16), NT,
        )
        e_a, e_b = jnp.exp(s_a), jnp.exp(s_b)
        if mask is not None:
            e_a, e_b = e_a * mask, e_b * mask
        e = jnp.concatenate([e_a, e_b], 0)
        eh, el = split(e)
        vh, vl = split(v[:, at])
        o = dot(eh, jnp.concatenate([vh, vl], 1))
        o = o[:, :pair] + (o[:, pair:] + dot(el, vh))
        o = o / jnp.sum(e, -1, keepdims=True)
        mixed.append(jnp.where(first, o[:rows], o[rows:]))
    return x + product(jnp.concatenate(mixed, 1), w_out)


def body(
    n,
    parts,
    video,
    starts,
    gain_space,
    qkv_space,
    out_space,
    gain_time,
    qkv_time,
    out_time,
    code_sums,
    code_counts,
    latents,
    terms,
    spaced,
    xin,
    codes,
    tok,
    weights,
    unit,
    warm,
    total,
    den,
    counted,
    part_sums,
    arrived,
    a2a_send,
    a2a_recv,
    g_send,
    g_recv,
    t_send,
    t_recv,
    d_send,
    d_recv,
    r_send,
    r_recv,
):
    clips, places, width = video.shape
    share = places // n
    pieces = xin.shape[1]
    rows = code_sums.shape[0]
    blocks = codes.shape[0]
    mates = tok.shape[1]
    stages = blocks.bit_length() - 1
    tokens = mates * places
    chunk, part, lanes = rows // 4, rows // parts, 128
    code_bits = [1] + list(range(3, n.bit_length() - 1))

    me = lax.axis_index("frames")
    pending = []

    def flip(k):
        return (1 - 2 * ((me // 2**k) % 2)) * 2**k

    def token_mate(k):
        return me + (k & 1) * flip(0) + (k >> 1) * flip(2)

    def block_mate(r):
        to = me
        for j in range(stages):
            if (r >> j) & 1:
                to = to + flip(code_bits[j])
        return to

    def remote(src, dst, ssem, rsem, dev):
        return pltpu.make_async_remote_copy(
            src_ref=src, dst_ref=dst, send_sem=ssem, recv_sem=rsem,
            device_id={"frames": dev}, device_id_type=pl.DeviceIdType.MESH,
        )

    def send(src, dst, ssem, rsem, dev):
        cp = remote(src, dst, ssem, rsem, dev)
        cp.start()
        pending.append(cp)

    barrier = pltpu.get_barrier_semaphore()

    def greet(i, c):
        pl.semaphore_signal(
            barrier, inc=1, device_id={"frames": lax.rem(me + i, n)},
            device_id_type=pl.DeviceIdType.MESH,
        )
        return c

    lax.fori_loop(1, n, greet, 0)

    own = code_sums[...] / jnp.transpose(jnp.broadcast_to(code_counts[...], (width, rows)))
    codes[0] = own * lax.rsqrt(jnp.sum(own * own, -1, keepdims=True) + EPSILON)
    pl.semaphore_wait(barrier, n - 1)

    def code_copy(r, q, ch, dev):
        at = pl.ds(ch * chunk, chunk)
        return remote(codes.at[r, at], codes.at[q, at], g_send.at[q, ch], g_recv.at[q, ch], dev)

    def give_codes(r, j, ch):
        cp = code_copy(r, r ^ (1 << j), ch, block_mate(1 << j))
        cp.start()
        pending.append(cp)

    def await_codes(r, chs):
        for ch in chs:
            code_copy(r, r, ch, me).wait_recv()

    def pass_codes(chs):
        for j in range(1, stages):
            for r in range(1 << j, 2 << j, 2):
                for ch in chs:
                    await_codes(r, [ch])
                    for i in range(j + 1, stages):
                        give_codes(r, i, ch)
                    give_codes(r, 0, ch)

    def token_copy(c, h, q, p, dev):
        at = pl.ds(h * (places // pieces), places // pieces)
        return remote(tok.at[c, q, at], tok.at[c, p, at], t_send.at[c, h, p], t_recv.at[c, h, p], dev)

    def give_tokens(c, h, q, k, dev):
        cp = token_copy(c, h, q, q ^ k, dev)
        cp.start()
        pending.append(cp)

    def await_tokens(c, h, q):
        token_copy(c, h, q, q, me).wait_recv()

    early, late = [0], [1, 2, 3]
    for ch in early + late:
        give_codes(0, 0, ch)
    for ch in early:
        for j in range(1, stages):
            give_codes(0, j, ch)

    w_q, w_o = split(qkv_space[...]), split(out_space[...])
    gain = gain_space[...]
    def deal(c, h, d):
        to = lax.rem(me + d, n)
        send(
            spaced.at[c, pl.ds(pl.multiple_of(to * share + h * places // n // pieces, 8), share // pieces), :],
            xin.at[c, h, me], a2a_send.at[c, h, d], a2a_recv.at[c, h, d], to,
        )

    def await_deal(c, h, d):
        src = lax.rem(me + n - d, n)
        remote(xin.at[c, h, src], xin.at[c, h, src], a2a_send.at[c, h, d], a2a_recv.at[c, h, d], me).wait_recv()

    def keep(c):
        for h in range(pieces):
            at = pl.ds(pl.multiple_of(me * share + h * places // n // pieces, 8), share // pieces)
            xin[c, h, me] = spaced[c, at, :]

    units = [(c, h) for c in range(clips) for h in range(pieces)]
    for c in range(clips):
        spaced[c] = attention(video[c], gain, w_q, w_o, None)
        if c < 2:
            for d in range(1, n):
                deal(*units[c], d)
        keep(c)

    def ready(c, h):
        for q in (2 * h, 2 * h + 1):
            if q % 2:
                for i in range(pieces):
                    await_tokens(c, i, q)
            u = tok[c, q]
            at = pl.ds((c * mates + q) * places, places)
            unit[at, :] = u.astype(BF16)
            warm[0, at, :], warm[1, at, :] = split(u * (1.0 / SOFTMAX_WARMTH))

    def score(c, h, r):
        two = 2 * places
        at = pl.ds(c * tokens + h * two, two)
        e = jnp.exp(dot3(split(codes[r]), (warm[0, at, :], warm[1, at, :]), NT))
        at = pl.ds(h * two, two)
        weights[c, r, :, at] = e
        t = jnp.sum(e.reshape(rows // 8, 8, two), 0)
        total[c, :, at] = t if r == 0 else total[c, :, at] + t

    def share_totals(c):
        den[c, 0] = jnp.sum(total[c], 0, keepdims=True)
        for k in range(1, mates):
            send(den.at[c, 0], den.at[c, k], d_send.at[c, k], d_recv.at[c, k], token_mate(k))

    def inverse_totals(c):
        for k in range(1, mates):
            remote(den.at[c, k], den.at[c, k], d_send.at[c, k], d_recv.at[c, k], me).wait_recv()
        full = [
            sum(den[c, k, :, pl.ds((q ^ k) * places, places)] for k in range(mates)) for q in range(mates)
        ]
        return 1.0 / jnp.concatenate(full, 1)

    w_q, w_o = split(qkv_time[...]), split(out_time[...])
    gain = gain_time[...]
    block = places // pieces
    bits = (share // pieces).bit_length() - 1
    r_i = lax.broadcasted_iota(jnp.int32, (block, block), 0)
    r_j = lax.broadcasted_iota(jnp.int32, (block, block), 1)
    t_i, t_j = r_i >> bits, r_j >> bits
    same_place = (r_i & (share // pieces - 1)) == (r_j & (share // pieces - 1))

    def pass_tokens(c, h):
        await_tokens(c, h, 2)
        give_tokens(c, h, 2, 1, token_mate(1))

    def late_codes():
        for ch in late:
            for j in range(1, stages):
                give_codes(0, j, ch)

    for i, (c, h) in enumerate(units):
        for d in range(1, n):
            await_deal(c, h, d)
            if i + 2 < len(units):
                deal(*units[i + 2], d)
        allowed = same_place & (t_j <= t_i) & ((t_j >= starts[c]) | (t_j == t_i))
        mask = jnp.where(allowed, 1.0, 0.0)
        y = attention(xin[c, h].reshape(block, width), gain, w_q, w_o, mask)
        each = share // pieces
        latents[c, :, pl.ds(h * each, each), :] = y.reshape(n, each, width)
        tok[c, 0, pl.ds(h * block, block), :] = y * lax.rsqrt(jnp.sum(y * y, -1, keepdims=True) + EPSILON)
        give_tokens(c, h, 0, 2, token_mate(2))
        give_tokens(c, h, 0, 1, token_mate(1))
        if i >= 2:
            pass_tokens(*units[i - 2])
        if i == 0:
            late_codes()
    pass_codes(early)
    for i in range(len(units) - 2, len(units)):
        if units[i][0] == 0:
            pass_tokens(*units[i])
    ready(0, 0)
    await_codes(1, early + late)
    score(0, 0, 0)
    score(0, 0, 1)
    ready(1, 0)
    score(1, 0, 0)
    score(1, 0, 1)
    ready(0, 1)
    score(0, 1, 0)
    score(0, 1, 1)
    pass_codes(late)
    evens = range(2, blocks, 2)
    odds = range(3, blocks, 2)
    for r in evens:
        for c, h in ((0, 0), (0, 1), (1, 0)):
            score(c, h, r)
    for i in range(len(units) - 2, len(units)):
        if units[i][0]:
            pass_tokens(*units[i])
    for r in odds:
        await_codes(r, early + late)
        for c, h in ((0, 0), (0, 1), (1, 0)):
            score(c, h, r)
    share_totals(0)
    ready(1, 1)
    for r in range(blocks):
        score(1, 1, r)
    share_totals(1)
    ones = jnp.ones((8, lanes), BF16)

    def term(c, r, h, inv):
        first, size = h * part, part
        p = weights[c, r, pl.ds(first, size), :] * inv
        at = pl.ds(c * tokens, tokens)
        sums = dot(p.astype(BF16), unit[at, :])
        k = p[:, :lanes]
        for i in range(1, tokens // lanes):
            k = k + p[:, i * lanes : (i + 1) * lanes]
        at = pl.ds(first, size)
        if c:
            sums = part_sums[r, at, :] + sums
            k = counted[r, at, :] + k
        part_sums[r, at, :] = sums
        counted[r, at, :] = k
        if c == clips - 1 and first + size == rows:
            kh, kl = split(counted[r])
            cnt = dot(ones, kh, NT) + dot(ones, kl, NT)
            if rows < width:
                cnt = jnp.concatenate([cnt, jnp.zeros((8, width - rows), F32)], 1)
            part_sums[r, pl.ds(rows, 8), :] = cnt

    def stage_of(r):
        j = 0
        while j < stages and not (r >> j) & 1:
            j += 1
        return j

    def slot(r, j):
        return (blocks - (blocks >> j)) + (r >> (j + 1))

    order = sorted(range(blocks), key=lambda r: (stage_of(r), -r))
    inv = inverse_totals(0)
    for c in range(clips - 1):
        for r in order:
            for h in range(parts):
                term(c, r, h, inv)
        inv = inverse_totals(c + 1)
    for r in order:
        k = stage_of(r)
        for h in range(parts):
            term(clips - 1, r, h, inv)
            at = pl.ds(h * part, part + (8 if h == parts - 1 else 0))
            for j in range(k):
                i = slot(r, j)
                remote(arrived.at[i, at], arrived.at[i, at], r_send.at[i, h], r_recv.at[i, h], me).wait_recv()
                part_sums[r, at, :] = part_sums[r, at, :] + arrived[i, at, :]
            if r:
                i = slot(r ^ (1 << k), k)
                send(part_sums.at[r, at], arrived.at[i, at], r_send.at[i, h], r_recv.at[i, h], block_mate(1 << k))
            else:
                terms[at, :] = part_sums[r, at, :]
    for cp in pending:
        cp.wait_send()


def finish(found, terms, code_sums, code_counts, latents, new_sums, new_counts, new_codebook):
    rows, width = code_sums.shape
    latents[...] = found[...]
    sums = DECAY_RATE * code_sums[...] + (1.0 - DECAY_RATE) * terms[:rows, :]
    counts = DECAY_RATE * code_counts[...] + (1.0 - DECAY_RATE) * terms[rows : rows + 1, :rows]
    new_sums[...] = sums
    new_counts[...] = counts
    new_codebook[...] = sums / jnp.transpose(jnp.broadcast_to(counts, (width, rows)))


def local(n, video, clip_start, gain_space, qkv_space, out_space, gain_time, qkv_time, out_time, code_sums, code_counts):
    clips, _, places, width = video.shape
    rows = code_sums.shape[0]
    share, blocks, mates = places // n, n // 4, 4
    parts = max(1, rows // 64)
    pieces = 1
    tokens = mates * places
    vmem = pl.BlockSpec(memory_space=pltpu.VMEM)
    dma = pltpu.SemaphoreType.DMA
    found, terms = pl.pallas_call(
        functools.partial(body, n, parts),
        out_shape=(
            jax.ShapeDtypeStruct((clips, n, share, width), F32),
            jax.ShapeDtypeStruct((rows + 8, width), F32),
        ),
        in_specs=[vmem, pl.BlockSpec(memory_space=pltpu.SMEM)] + [vmem] * 8,
        out_specs=(vmem,) * 2,
        scratch_shapes=[
            pltpu.VMEM((clips, places, width), F32),
            pltpu.VMEM((clips, pieces, n, share // pieces, width), F32),
            pltpu.VMEM((blocks, rows, width), F32),
            pltpu.VMEM((clips, mates, places, width), F32),
            pltpu.VMEM((clips, blocks, rows, tokens), F32),
            pltpu.VMEM((clips * tokens, width), BF16),
            pltpu.VMEM((2, clips * tokens, width), BF16),
            pltpu.VMEM((clips, 8, tokens), F32),
            pltpu.VMEM((clips, mates, 1, tokens), F32),
            pltpu.VMEM((blocks, rows, 128), F32),
            pltpu.VMEM((blocks, rows + 8, width), F32),
            pltpu.VMEM((blocks, rows + 8, width), F32),
            dma((clips, pieces, n)), dma((clips, pieces, n)),
            dma((blocks, 4)), dma((blocks, 4)),
            dma((clips, pieces, mates)), dma((clips, pieces, mates)),
            dma((clips, mates)), dma((clips, mates)),
            dma((blocks, parts)), dma((blocks, parts)),
        ],
        compiler_params=pltpu.CompilerParams(
            collective_id=0, has_side_effects=True, vmem_limit_bytes=60 * 2**20
        ),
        name="tokenizer",
    )(
        video.reshape(clips, places, width), clip_start, gain_space.reshape(1, -1), qkv_space, out_space,
        gain_time.reshape(1, -1), qkv_time, out_time, code_sums, code_counts.reshape(1, -1),
    )
    lat, sums, counts, book = pl.pallas_call(
        finish,
        out_shape=(
            jax.ShapeDtypeStruct((clips, n, share, width), F32),
            jax.ShapeDtypeStruct((rows, width), F32),
            jax.ShapeDtypeStruct((1, rows), F32),
            jax.ShapeDtypeStruct((rows, width), F32),
        ),
        in_specs=[vmem] * 4,
        out_specs=(vmem,) * 4,
        name="finish",
    )(found, terms, code_sums, code_counts.reshape(1, -1))
    return lat, sums, counts.reshape(rows), book


def solution(mesh):
    in_specs = (
        P("groups", "frames", None, None),
        P("groups"),
        P(),
        P(),
        P(),
        P(),
        P(),
        P(),
        P(("groups", "frames"), None),
        P(("groups", "frames")),
    )
    out_specs = (
        P("groups", None, "frames", None),
        P(("groups", "frames"), None),
        P(("groups", "frames")),
        P(("groups", "frames"), None),
    )
    fn = functools.partial(local, mesh.shape["frames"])
    return jax.shard_map(fn, mesh=mesh, in_specs=in_specs, out_specs=out_specs, check_vma=False)
```

```python
import functools

import jax
import jax.numpy as jnp
from jax import lax
from jax.experimental import pallas as pl
from jax.experimental.pallas import tpu as pltpu
from jax.sharding import PartitionSpec as P

HEADS = 4
ATTN_SCALE = 10.0
SOFTMAX_WARMTH = 0.05
DECAY_RATE = 0.9
EPSILON = 1e-06
F32 = jnp.float32
BF16 = jnp.bfloat16
NN = (((1,), (0,)), ((), ()))
NT = (((1,), (1,)), ((), ()))


def split(a):
    hi = a.astype(BF16)
    return hi, (a - hi.astype(F32)).astype(BF16)


def dot(a, b, dims=NN):
    return lax.dot_general(a, b, dims, preferred_element_type=F32)


def dot3(a, b, dims=NN):
    return dot(a[0], b[0], dims) + (dot(a[0], b[1], dims) + dot(a[1], b[0], dims))


def dot2(a, b, dims=NN):
    return dot(a[0], b, dims) + dot(a[1], b, dims)


def attention(x, gain, w_qkv, w_out, mask, between=None):
    rows, width = x.shape
    hd = width // HEADS
    pair = 2 * hd
    lane_i = lax.broadcasted_iota(jnp.int32, (width, width), 0) // hd
    lane_j = lax.broadcasted_iota(jnp.int32, (width, width), 1) // hd
    same_head = jnp.where(lane_i == lane_j, 1.0, 0.0).astype(BF16)
    first = lax.broadcasted_iota(jnp.int32, (rows, pair), 1) < hd

    def product(a, w):
        ah, al = split(a)
        both = dot(jnp.concatenate([ah, al], 0), w[0])
        return both[:rows] + (both[rows:] + dot(ah, w[1]))

    normed = x * lax.rsqrt(jnp.mean(x * x, -1, keepdims=True) + EPSILON) * gain
    packed = product(normed, w_qkv)
    q, k, v = packed[:, :width], packed[:, width : 2 * width], packed[:, 2 * width :]
    squares = dot(jnp.concatenate(split(q * q) + split(k * k), 0), same_head)
    q = q * lax.rsqrt(squares[:rows] + squares[rows : 2 * rows] + EPSILON) * ATTN_SCALE
    k = k * lax.rsqrt(squares[2 * rows : 3 * rows] + squares[3 * rows :] + EPSILON)
    if between is not None:
        between()
    mixed = []
    for p in range(HEADS // 2):
        at = slice(p * pair, (p + 1) * pair)
        qh = q[:, at].astype(BF16).astype(F32)
        kh = k[:, at].astype(BF16).astype(F32)
        ql = pltpu.roll(q[:, at] - qh, hd, 1)
        kr = pltpu.roll(kh, hd, 1)
        kl = k[:, at] - kh
        s_a = dot(
            jnp.concatenate([jnp.where(first, qh, ql), jnp.where(first, qh, 0.0)], 1).astype(BF16),
            jnp.concatenate([jnp.where(first, kh, kr), kl], 1).astype(BF16), NT,
        )
        s_b = dot(
            jnp.concatenate([jnp.where(first, ql, qh), jnp.where(first, 0.0, qh)], 1).astype(BF16),
            jnp.concatenate([jnp.where(first, kr, kh), kl], 1).astype(BF16), NT,
        )
        e_a, e_b = jnp.exp(s_a), jnp.exp(s_b)
        if mask is not None:
            e_a, e_b = e_a * mask, e_b * mask
        e = jnp.concatenate([e_a, e_b], 0)
        eh, el = split(e)
        vh, vl = split(v[:, at])
        o = dot(eh, jnp.concatenate([vh, vl], 1))
        o = o[:, :pair] + (o[:, pair:] + dot(el, vh))
        o = o / jnp.sum(e, -1, keepdims=True)
        mixed.append(jnp.where(first, o[:rows], o[rows:]))
    return x + product(jnp.concatenate(mixed, 1), w_out)


def body(
    n,
    spans,
    video_in,
    starts,
    gain_space,
    qkv_space_in,
    out_space_in,
    gain_time,
    qkv_time_in,
    out_time_in,
    code_sums_in,
    code_counts,
    latents_out,
    terms_out,
    video,
    qkv_space,
    out_space,
    qkv_time,
    out_time,
    code_sums,
    latents,
    in_sem,
    lat_sem,
    out_sem,
    spaced,
    xin,
    codes,
    tok,
    weights,
    unit,
    warm,
    total,
    den,
    counted,
    part_sums,
    arrived,
    a2a_send,
    a2a_recv,
    g_send,
    g_recv,
    t_send,
    t_recv,
    d_send,
    d_recv,
    r_send,
    r_recv,
):
    clips, places, width = video.shape
    share = places // n
    pieces = xin.shape[1]
    rows = code_sums.shape[0]
    blocks = codes.shape[0]
    mates = tok.shape[1]
    stages = blocks.bit_length() - 1
    tokens = mates * places
    chunk, lanes = rows // 4, 128
    parts, swapped = len(spans), 1 if stages > 1 else 0
    code_bits = [1] + list(range(3, n.bit_length() - 1))

    me = lax.axis_index("frames")
    pending = []

    def flip(k):
        return (1 - 2 * ((me // 2**k) % 2)) * 2**k

    def token_mate(k):
        return me + (k & 1) * flip(0) + (k >> 1) * flip(2)

    def block_mate(r):
        to = me
        for j in range(stages):
            if (r >> j) & 1:
                to = to + flip(code_bits[j])
        return to

    def remote(src, dst, ssem, rsem, dev):
        return pltpu.make_async_remote_copy(
            src_ref=src, dst_ref=dst, send_sem=ssem, recv_sem=rsem,
            device_id={"frames": dev}, device_id_type=pl.DeviceIdType.MESH,
        )

    def send(src, dst, ssem, rsem, dev):
        cp = remote(src, dst, ssem, rsem, dev)
        cp.start()
        pending.append(cp)

    barrier = pltpu.get_barrier_semaphore()

    def greet(i, c):
        pl.semaphore_signal(
            barrier, inc=1, device_id={"frames": lax.rem(me + i, n)},
            device_id_type=pl.DeviceIdType.MESH,
        )
        return c

    lax.fori_loop(1, n, greet, 0)
    loads = {}
    for i, (name, src, dst) in enumerate((
        ("video0", video_in.at[0], video.at[0]), ("qkv_space", qkv_space_in, qkv_space),
        ("out_space", out_space_in, out_space), ("code_sums", code_sums_in, code_sums),
        ("video1", video_in.at[pl.ds(1, clips - 1)], video.at[pl.ds(1, clips - 1)]),
        ("qkv_time", qkv_time_in, qkv_time), ("out_time", out_time_in, out_time),
    )):
        loads[name] = pltpu.make_async_copy(src, dst, in_sem.at[i])
        loads[name].start()

    def code_copy(r, q, ch, dev):
        at = pl.ds(ch * chunk, chunk)
        return remote(codes.at[r, at], codes.at[q, at], g_send.at[q, ch], g_recv.at[q, ch], dev)

    def give_codes(r, j, ch):
        cp = code_copy(r, r ^ (1 << j), ch, block_mate(1 << j))
        cp.start()
        pending.append(cp)

    def await_codes(r, chs):
        for ch in chs:
            code_copy(r, r, ch, me).wait_recv()

    def pass_codes(chs):
        for j in range(1, stages):
            for r in range(1 << j, 2 << j, 2):
                for ch in chs:
                    await_codes(r, [ch])
                    for i in range(j + 1, stages):
                        give_codes(r, i, ch)
                    give_codes(r, 0, ch)

    def token_copy(c, h, q, p, dev):
        at = pl.ds(h * (places // pieces), places // pieces)
        return remote(tok.at[c, q, at], tok.at[c, p, at], t_send.at[c, h, p], t_recv.at[c, h, p], dev)

    def give_tokens(c, h, q, k, dev):
        cp = token_copy(c, h, q, q ^ k, dev)
        cp.start()
        pending.append(cp)

    def await_tokens(c, h, q):
        token_copy(c, h, q, q, me).wait_recv()

    code_at = [-2, -2, 0, 0]
    early = [ch for ch in range(4) if code_at[ch] < 0]
    late = [ch for ch in range(4) if code_at[ch] >= 0]

    def across(when):
        for ch in range(4 if when == -2 else 0):
            give_codes(0, 0, ch)
        for ch in range(4):
            if code_at[ch] == when:
                for j in range(1, stages):
                    give_codes(0, j, ch)

    def enter():
        loads["code_sums"].wait()
        own = code_sums[...] / jnp.transpose(jnp.broadcast_to(code_counts[...], (width, rows)))
        codes[0] = own * lax.rsqrt(jnp.sum(own * own, -1, keepdims=True) + EPSILON)
        pl.semaphore_wait(barrier, n - 1)
        across(-2)

    loads["qkv_space"].wait()
    loads["out_space"].wait()
    w_q, w_o = split(qkv_space[...]), split(out_space[...])
    gain = gain_space[...]
    def deal(c, h, d):
        to = lax.rem(me + d, n)
        send(
            spaced.at[c, pl.ds(pl.multiple_of(to * share + h * places // n // pieces, 8), share // pieces), :],
            xin.at[c, h, me], a2a_send.at[c, h, d], a2a_recv.at[c, h, d], to,
        )

    def await_deal(c, h, d):
        src = lax.rem(me + n - d, n)
        remote(xin.at[c, h, src], xin.at[c, h, src], a2a_send.at[c, h, d], a2a_recv.at[c, h, d], me).wait_recv()

    def keep(c):
        for h in range(pieces):
            at = pl.ds(pl.multiple_of(me * share + h * places // n // pieces, 8), share // pieces)
            xin[c, h, me] = spaced[c, at, :]

    units = [(c, h) for c in range(clips) for h in range(pieces)]
    for c in range(clips):
        if c < 2:
            loads["video%d" % c].wait()
        spaced[c] = attention(video[c], gain, w_q, w_o, None, enter if c == 0 else None)
        if c < 1:
            for d in range(1, n):
                deal(*units[c], d)
        keep(c)
    across(-1)
    loads["qkv_time"].wait()
    loads["out_time"].wait()

    def ready(c, h):
        for q in (2 * h, 2 * h + 1):
            if q % 2:
                for i in range(pieces):
                    await_tokens(c, i, q)
            u = tok[c, q]
            at = pl.ds((c * mates + q) * places, places)
            unit[at, :] = u.astype(BF16)
            warm[0, at, :], warm[1, at, :] = split(u * (1.0 / SOFTMAX_WARMTH))

    def score(c, h, r):
        two = 2 * places
        at = pl.ds(c * tokens + h * two, two)
        e = jnp.exp(dot3(split(codes[r]), (warm[0, at, :], warm[1, at, :]), NT))
        at = pl.ds(h * two, two)
        weights[c, r, :, at] = e
        t = jnp.sum(e.reshape(rows // 8, 8, two), 0)
        total[c, :, at] = t if r == 0 else total[c, :, at] + t

    def share_totals(c):
        den[c, 0] = jnp.sum(total[c], 0, keepdims=True)
        for k in range(1, mates):
            send(den.at[c, 0], den.at[c, k], d_send.at[c, k], d_recv.at[c, k], token_mate(k))

    def inverse_totals(c):
        for k in range(1, mates):
            remote(den.at[c, k], den.at[c, k], d_send.at[c, k], d_recv.at[c, k], me).wait_recv()
        full = [
            sum(den[c, k, :, pl.ds((q ^ k) * places, places)] for k in range(mates)) for q in range(mates)
        ]
        return 1.0 / jnp.concatenate(full, 1)

    w_q, w_o = split(qkv_time[...]), split(out_time[...])
    gain = gain_time[...]
    block = places // pieces
    bits = (share // pieces).bit_length() - 1
    r_i = lax.broadcasted_iota(jnp.int32, (block, block), 0)
    r_j = lax.broadcasted_iota(jnp.int32, (block, block), 1)
    t_i, t_j = r_i >> bits, r_j >> bits
    same_place = (r_i & (share // pieces - 1)) == (r_j & (share // pieces - 1))

    def pass_tokens(c, h):
        await_tokens(c, h, 2)
        give_tokens(c, h, 2, 1, token_mate(1))

    saves = []
    for i, (c, h) in enumerate(units):
        for d in range(1, n):
            await_deal(c, h, d)
            if i + 1 < len(units):
                deal(*units[i + 1], d)
        allowed = same_place & (t_j <= t_i) & ((t_j >= starts[c]) | (t_j == t_i))
        mask = jnp.where(allowed, 1.0, 0.0)
        y = attention(xin[c, h].reshape(block, width), gain, w_q, w_o, mask)
        each = share // pieces
        latents[c, :, pl.ds(h * each, each), :] = y.reshape(n, each, width)
        tok[c, 0, pl.ds(h * block, block), :] = y * lax.rsqrt(jnp.sum(y * y, -1, keepdims=True) + EPSILON)
        give_tokens(c, h, 0, 2, token_mate(2))
        give_tokens(c, h, 0, 1, token_mate(1))
        if i >= 2:
            pass_tokens(*units[i - 2])
        if h == pieces - 1:
            saves.append(pltpu.make_async_copy(latents.at[c], latents_out.at[c], lat_sem.at[c]))
            saves[-1].start()
        across(i)
    pass_codes(early)
    ready(0, 0)
    await_codes(1, early + late)
    score(0, 0, 0)
    score(0, 0, 1)
    ready(1, 0)
    score(1, 0, 0)
    score(1, 0, 1)
    for i in range(len(units) - 2, len(units)):
        if units[i][0] == 0:
            pass_tokens(*units[i])
    pass_codes(late)
    evens = range(2, blocks, 2)
    odds = range(3, blocks, 2)
    for r in evens:
        score(0, 0, r)
        score(1, 0, r)
    ready(0, 1)
    for r in (0, 1, *evens):
        score(0, 1, r)
    for i in range(len(units) - 2, len(units)):
        if units[i][0]:
            pass_tokens(*units[i])
    for r in odds:
        await_codes(r, early + late)
        score(0, 0, r)
        score(0, 1, r)
    share_totals(0)
    for r in odds:
        score(1, 0, r)
    ready(1, 1)
    for r in range(blocks):
        score(1, 1, r)
    share_totals(1)
    ones = jnp.ones((8, lanes), BF16)

    def term(c, r, h, inv):
        first, size = spans[h]
        p = weights[c, r, pl.ds(first, size), :] * inv
        at = pl.ds(c * tokens, tokens)
        sums = dot(p.astype(BF16), unit[at, :])
        k = p[:, :lanes]
        for i in range(1, tokens // lanes):
            k = k + p[:, i * lanes : (i + 1) * lanes]
        at = pl.ds(first, size)
        if c:
            sums = part_sums[r, at, :] + sums
            k = counted[r, at, :] + k
        part_sums[r, at, :] = sums
        counted[r, at, :] = k
        if c == clips - 1 and first + size == rows:
            kh, kl = split(counted[r])
            cnt = dot(ones, kh, NT) + dot(ones, kl, NT)
            if rows < width:
                cnt = jnp.concatenate([cnt, jnp.zeros((8, width - rows), F32)], 1)
            part_sums[r, pl.ds(rows, 8), :] = cnt

    def route(h):
        bits = list(range(stages))
        return bits[1::-1] + bits[2:] if h < swapped else bits

    def stage_of(r, h):
        k = 0
        while k < stages and not (r >> route(h)[k]) & 1:
            k += 1
        return k

    def slot(r, k, h):
        cleared = [sum(1 << j for j in route(h)[: i + 1]) for i in range(stages)]
        places_at = [(i, q) for i in range(stages) for q in range(blocks) if not q & cleared[i]]
        return places_at.index((k, r))

    inv = {}
    made = set()

    def make(r, h, c):
        if (r, h, c) not in made:
            made.add((r, h, c))
            if h == parts - 1 and c == clips - 1:
                for g in range(h):
                    make(r, g, c)
            for b in range(c):
                make(r, h, b)
            if c not in inv:
                inv[c] = inverse_totals(c)
            term(c, r, h, inv[c])

    jobs = [(r, h) for r in range(blocks) for h in range(parts)]
    jobs.sort(key=lambda job: (stage_of(*job), -(job[1] < swapped) if stage_of(*job) == 0 else job[1] < swapped, -job[0], job[1]))
    for r, h in jobs[: 2 * parts]:
        make(r, h, 0)
    for r, h in jobs:
        make(r, h, clips - 1)
        k = stage_of(r, h)
        first, size = spans[h]
        at = pl.ds(first, size + (8 if h == parts - 1 else 0))
        for j in range(k):
            i = slot(r, j, h)
            remote(arrived.at[i, at], arrived.at[i, at], r_send.at[i, h], r_recv.at[i, h], me).wait_recv()
            part_sums[r, at, :] = part_sums[r, at, :] + arrived[i, at, :]
        if r:
            j = route(h)[k]
            i = slot(r ^ (1 << j), k, h)
            send(part_sums.at[r, at], arrived.at[i, at], r_send.at[i, h], r_recv.at[i, h], block_mate(1 << j))
        else:
            saves.append(pltpu.make_async_copy(part_sums.at[r, at], terms_out.at[at], out_sem.at[h]))
            saves[-1].start()
    for cp in pending:
        cp.wait_send()
    for cp in saves:
        cp.wait()


def finish(found, terms, code_sums, code_counts, latents, new_sums, new_counts, new_codebook):
    rows, width = code_sums.shape
    latents[...] = found[...]
    sums = DECAY_RATE * code_sums[...] + (1.0 - DECAY_RATE) * terms[:rows, :]
    counts = DECAY_RATE * code_counts[...] + (1.0 - DECAY_RATE) * terms[rows : rows + 1, :rows]
    new_sums[...] = sums
    new_counts[...] = counts
    new_codebook[...] = sums / jnp.transpose(jnp.broadcast_to(counts, (width, rows)))


def local(n, video, clip_start, gain_space, qkv_space, out_space, gain_time, qkv_time, out_time, code_sums, code_counts):
    clips, _, places, width = video.shape
    rows = code_sums.shape[0]
    share, blocks, mates = places // n, n // 4, 4
    sizes = [32, 32] + [64] * (rows // 64 - 1)
    spans = [(sum(sizes[:i]), z) for i, z in enumerate(sizes)]
    parts = len(spans)
    pieces = 1
    tokens = mates * places
    vmem = pl.BlockSpec(memory_space=pltpu.VMEM)
    hbm = pl.BlockSpec(memory_space=pl.ANY)
    dma = pltpu.SemaphoreType.DMA
    found, terms = pl.pallas_call(
        functools.partial(body, n, spans),
        out_shape=(
            jax.ShapeDtypeStruct((clips, n, share, width), F32),
            jax.ShapeDtypeStruct((rows + 8, width), F32),
        ),
        in_specs=[hbm, pl.BlockSpec(memory_space=pltpu.SMEM), vmem, hbm, hbm, vmem, hbm, hbm, hbm, vmem],
        out_specs=(hbm,) * 2,
        scratch_shapes=[
            pltpu.VMEM((clips, places, width), F32),
            pltpu.VMEM((width, 3 * width), F32),
            pltpu.VMEM((width, width), F32),
            pltpu.VMEM((width, 3 * width), F32),
            pltpu.VMEM((width, width), F32),
            pltpu.VMEM((rows, width), F32),
            pltpu.VMEM((clips, n, share, width), F32),
            dma((7,)), dma((clips,)), dma((parts,)),
            pltpu.VMEM((clips, places, width), F32),
            pltpu.VMEM((clips, pieces, n, share // pieces, width), F32),
            pltpu.VMEM((blocks, rows, width), F32),
            pltpu.VMEM((clips, mates, places, width), F32),
            pltpu.VMEM((clips, blocks, rows, tokens), F32),
            pltpu.VMEM((clips * tokens, width), BF16),
            pltpu.VMEM((2, clips * tokens, width), BF16),
            pltpu.VMEM((clips, 8, tokens), F32),
            pltpu.VMEM((clips, mates, 1, tokens), F32),
            pltpu.VMEM((blocks, rows, 128), F32),
            pltpu.VMEM((blocks, rows + 8, width), F32),
            pltpu.VMEM((blocks, rows + 8, width), F32),
            dma((clips, pieces, n)), dma((clips, pieces, n)),
            dma((blocks, 4)), dma((blocks, 4)),
            dma((clips, pieces, mates)), dma((clips, pieces, mates)),
            dma((clips, mates)), dma((clips, mates)),
            dma((blocks, parts)), dma((blocks, parts)),
        ],
        compiler_params=pltpu.CompilerParams(
            collective_id=0, has_side_effects=True, vmem_limit_bytes=60 * 2**20
        ),
        name="tokenizer",
    )(
        video.reshape(clips, places, width), clip_start, gain_space.reshape(1, -1), qkv_space, out_space,
        gain_time.reshape(1, -1), qkv_time, out_time, code_sums, code_counts.reshape(1, -1),
    )
    lat, sums, counts, book = pl.pallas_call(
        finish,
        out_shape=(
            jax.ShapeDtypeStruct((clips, n, share, width), F32),
            jax.ShapeDtypeStruct((rows, width), F32),
            jax.ShapeDtypeStruct((1, rows), F32),
            jax.ShapeDtypeStruct((rows, width), F32),
        ),
        in_specs=[vmem] * 4,
        out_specs=(vmem,) * 4,
        name="finish",
    )(found, terms, code_sums, code_counts.reshape(1, -1))
    return lat, sums, counts.reshape(rows), book


def solution(mesh):
    in_specs = (
        P("groups", "frames", None, None),
        P("groups"),
        P(),
        P(),
        P(),
        P(),
        P(),
        P(),
        P(("groups", "frames"), None),
        P(("groups", "frames")),
    )
    out_specs = (
        P("groups", None, "frames", None),
        P(("groups", "frames"), None),
        P(("groups", "frames")),
        P(("groups", "frames"), None),
    )
    fn = functools.partial(local, mesh.shape["frames"])
    return jax.shard_map(fn, mesh=mesh, in_specs=in_specs, out_specs=out_specs, check_vma=False)
```

```python
import functools

import jax
import jax.numpy as jnp
from jax import lax
from jax.experimental import pallas as pl
from jax.experimental.pallas import tpu as pltpu
from jax.sharding import PartitionSpec as P

HEADS = 4
ATTN_SCALE = 10.0
SOFTMAX_WARMTH = 0.05
DECAY_RATE = 0.9
EPSILON = 1e-06
F32 = jnp.float32
BF16 = jnp.bfloat16
NN = (((1,), (0,)), ((), ()))
NT = (((1,), (1,)), ((), ()))


def split(a):
    hi = a.astype(BF16)
    return hi, (a - hi.astype(F32)).astype(BF16)


def dot(a, b, dims=NN):
    return lax.dot_general(a, b, dims, preferred_element_type=F32)


def dot3(a, b, dims=NN):
    return dot(a[0], b[0], dims) + (dot(a[0], b[1], dims) + dot(a[1], b[0], dims))


def dot2(a, b, dims=NN):
    return dot(a[0], b, dims) + dot(a[1], b, dims)


def attention(x, gain, w_qkv, w_out, mask, between=None):
    rows, width = x.shape
    hd = width // HEADS
    pair = 2 * hd
    lane_i = lax.broadcasted_iota(jnp.int32, (width, width), 0) // hd
    lane_j = lax.broadcasted_iota(jnp.int32, (width, width), 1) // hd
    same_head = jnp.where(lane_i == lane_j, 1.0, 0.0).astype(BF16)
    first = lax.broadcasted_iota(jnp.int32, (rows, pair), 1) < hd

    def product(a, w):
        ah, al = split(a)
        both = dot(jnp.concatenate([ah, al], 0), w[0])
        return both[:rows] + (both[rows:] + dot(ah, w[1]))

    normed = x * lax.rsqrt(jnp.mean(x * x, -1, keepdims=True) + EPSILON) * gain
    packed = product(normed, w_qkv)
    q, k, v = packed[:, :width], packed[:, width : 2 * width], packed[:, 2 * width :]
    squares = dot(jnp.concatenate(split(q * q) + split(k * k), 0), same_head)
    q = q * lax.rsqrt(squares[:rows] + squares[rows : 2 * rows] + EPSILON) * ATTN_SCALE
    k = k * lax.rsqrt(squares[2 * rows : 3 * rows] + squares[3 * rows :] + EPSILON)
    if between is not None:
        between()
    mixed = []
    for p in range(HEADS // 2):
        at = slice(p * pair, (p + 1) * pair)
        qh = q[:, at].astype(BF16).astype(F32)
        kh = k[:, at].astype(BF16).astype(F32)
        ql = pltpu.roll(q[:, at] - qh, hd, 1)
        kr = pltpu.roll(kh, hd, 1)
        kl = k[:, at] - kh
        s_a = dot(
            jnp.concatenate([jnp.where(first, qh, ql), jnp.where(first, qh, 0.0)], 1).astype(BF16),
            jnp.concatenate([jnp.where(first, kh, kr), kl], 1).astype(BF16), NT,
        )
        s_b = dot(
            jnp.concatenate([jnp.where(first, ql, qh), jnp.where(first, 0.0, qh)], 1).astype(BF16),
            jnp.concatenate([jnp.where(first, kr, kh), kl], 1).astype(BF16), NT,
        )
        e_a, e_b = jnp.exp(s_a), jnp.exp(s_b)
        if mask is not None:
            e_a, e_b = e_a * mask, e_b * mask
        e = jnp.concatenate([e_a, e_b], 0)
        eh, el = split(e)
        vh, vl = split(v[:, at])
        o = dot(eh, jnp.concatenate([vh, vl], 1))
        o = o[:, :pair] + (o[:, pair:] + dot(el, vh))
        o = o / jnp.sum(e, -1, keepdims=True)
        mixed.append(jnp.where(first, o[:rows], o[rows:]))
    return x + product(jnp.concatenate(mixed, 1), w_out)


def body(
    n,
    spans,
    video_in,
    starts,
    gain_space,
    qkv_space_in,
    out_space_in,
    gain_time,
    qkv_time_in,
    out_time_in,
    code_sums_in,
    code_counts,
    latents_out,
    terms_out,
    video,
    qkv_space,
    out_space,
    qkv_time,
    out_time,
    code_sums,
    latents,
    in_sem,
    lat_sem,
    out_sem,
    spaced,
    xin,
    codes,
    tok,
    weights,
    unit,
    warm,
    total,
    den,
    counted,
    part_sums,
    arrived,
    a2a_send,
    a2a_recv,
    g_send,
    g_recv,
    t_send,
    t_recv,
    d_send,
    d_recv,
    r_send,
    r_recv,
):
    clips, places, width = video.shape
    share = places // n
    pieces = xin.shape[1]
    rows = code_sums.shape[0]
    blocks = codes.shape[0]
    mates = tok.shape[1]
    stages = blocks.bit_length() - 1
    tokens = mates * places
    chunk, lanes = rows // 4, 128
    parts, swapped = len(spans), 1 if stages > 1 else 0
    code_bits = [1] + list(range(3, n.bit_length() - 1))

    me = lax.axis_index("frames")
    pending = []

    def flip(k):
        return (1 - 2 * ((me // 2**k) % 2)) * 2**k

    def token_mate(k):
        return me + (k & 1) * flip(0) + (k >> 1) * flip(2)

    def block_mate(r):
        to = me
        for j in range(stages):
            if (r >> j) & 1:
                to = to + flip(code_bits[j])
        return to

    def remote(src, dst, ssem, rsem, dev):
        return pltpu.make_async_remote_copy(
            src_ref=src, dst_ref=dst, send_sem=ssem, recv_sem=rsem,
            device_id={"frames": dev}, device_id_type=pl.DeviceIdType.MESH,
        )

    def send(src, dst, ssem, rsem, dev):
        cp = remote(src, dst, ssem, rsem, dev)
        cp.start()
        pending.append(cp)

    barrier = pltpu.get_barrier_semaphore()

    def greet(i, c):
        pl.semaphore_signal(
            barrier, inc=1, device_id={"frames": lax.rem(me + i, n)},
            device_id_type=pl.DeviceIdType.MESH,
        )
        return c

    lax.fori_loop(1, n, greet, 0)
    loads = {}
    for i, (name, src, dst) in enumerate((
        ("video0", video_in.at[0], video.at[0]), ("qkv_space", qkv_space_in, qkv_space),
        ("out_space", out_space_in, out_space), ("code_sums", code_sums_in, code_sums),
        ("video1", video_in.at[pl.ds(1, clips - 1)], video.at[pl.ds(1, clips - 1)]),
        ("qkv_time", qkv_time_in, qkv_time), ("out_time", out_time_in, out_time),
    )):
        loads[name] = pltpu.make_async_copy(src, dst, in_sem.at[i])
        loads[name].start()

    def code_copy(r, q, ch, dev):
        at = pl.ds(ch * chunk, chunk)
        return remote(codes.at[r, at], codes.at[q, at], g_send.at[q, ch], g_recv.at[q, ch], dev)

    def give_codes(r, j, ch):
        cp = code_copy(r, r ^ (1 << j), ch, block_mate(1 << j))
        cp.start()
        pending.append(cp)

    def await_codes(r, chs):
        for ch in chs:
            code_copy(r, r, ch, me).wait_recv()

    def pass_codes(chs):
        for j in range(1, stages):
            for r in range(1 << j, 2 << j, 2):
                for ch in chs:
                    await_codes(r, [ch])
                    for i in range(j + 1, stages):
                        give_codes(r, i, ch)
                    give_codes(r, 0, ch)

    def token_copy(c, h, q, p, dev):
        at = pl.ds(h * (places // pieces), places // pieces)
        return remote(tok.at[c, q, at], tok.at[c, p, at], t_send.at[c, h, p], t_recv.at[c, h, p], dev)

    def give_tokens(c, h, q, k, dev):
        cp = token_copy(c, h, q, q ^ k, dev)
        cp.start()
        pending.append(cp)

    def await_tokens(c, h, q):
        token_copy(c, h, q, q, me).wait_recv()

    code_at = [-1, -1, 0, 0]
    early = [ch for ch in range(4) if code_at[ch] < 0]
    late = [ch for ch in range(4) if code_at[ch] >= 0]

    def across(when):
        for ch in range(4 if when == -2 else 0):
            give_codes(0, 0, ch)
        for ch in range(4):
            if code_at[ch] == when:
                for j in range(1, stages):
                    give_codes(0, j, ch)

    def enter():
        loads["code_sums"].wait()
        own = code_sums[...] / jnp.transpose(jnp.broadcast_to(code_counts[...], (width, rows)))
        codes[0] = own * lax.rsqrt(jnp.sum(own * own, -1, keepdims=True) + EPSILON)
        pl.semaphore_wait(barrier, n - 1)
        across(-2)

    loads["qkv_space"].wait()
    loads["out_space"].wait()
    w_q, w_o = split(qkv_space[...]), split(out_space[...])
    gain = gain_space[...]
    hops = sorted(range(1, n), key=lambda d: abs(2 * d - n))

    def deal(c, h, d):
        to = lax.rem(me + d, n)
        send(
            spaced.at[c, pl.ds(pl.multiple_of(to * share + h * places // n // pieces, 8), share // pieces), :],
            xin.at[c, h, me], a2a_send.at[c, h, d], a2a_recv.at[c, h, d], to,
        )

    def await_deal(c, h, d):
        src = lax.rem(me + n - d, n)
        remote(xin.at[c, h, src], xin.at[c, h, src], a2a_send.at[c, h, d], a2a_recv.at[c, h, d], me).wait_recv()

    def keep(c):
        for h in range(pieces):
            at = pl.ds(pl.multiple_of(me * share + h * places // n // pieces, 8), share // pieces)
            xin[c, h, me] = spaced[c, at, :]

    units = [(c, h) for c in range(clips) for h in range(pieces)]
    for c in range(clips):
        if c < 2:
            loads["video%d" % c].wait()
        spaced[c] = attention(video[c], gain, w_q, w_o, None, enter if c == 0 else None)
        if c < 1:
            for d in hops:
                deal(*units[c], d)
        keep(c)
    across(-1)
    loads["qkv_time"].wait()
    loads["out_time"].wait()

    def ready(c, h):
        for q in (2 * h, 2 * h + 1):
            if q % 2:
                for i in range(pieces):
                    await_tokens(c, i, q)
            u = tok[c, q]
            at = pl.ds((c * mates + q) * places, places)
            unit[at, :] = u.astype(BF16)
            warm[0, at, :], warm[1, at, :] = split(u * (1.0 / SOFTMAX_WARMTH))

    def score(c, h, r):
        two = 2 * places
        at = pl.ds(c * tokens + h * two, two)
        e = jnp.exp(dot3(split(codes[r]), (warm[0, at, :], warm[1, at, :]), NT))
        at = pl.ds(h * two, two)
        weights[c, r, :, at] = e
        t = jnp.sum(e.reshape(rows // 8, 8, two), 0)
        total[c, :, at] = t if r == 0 else total[c, :, at] + t

    def share_totals(c):
        den[c, 0] = jnp.sum(total[c], 0, keepdims=True)
        for k in range(1, mates):
            send(den.at[c, 0], den.at[c, k], d_send.at[c, k], d_recv.at[c, k], token_mate(k))

    def inverse_totals(c):
        for k in range(1, mates):
            remote(den.at[c, k], den.at[c, k], d_send.at[c, k], d_recv.at[c, k], me).wait_recv()
        full = [
            sum(den[c, k, :, pl.ds((q ^ k) * places, places)] for k in range(mates)) for q in range(mates)
        ]
        return 1.0 / jnp.concatenate(full, 1)

    w_q, w_o = split(qkv_time[...]), split(out_time[...])
    gain = gain_time[...]
    block = places // pieces
    bits = (share // pieces).bit_length() - 1
    r_i = lax.broadcasted_iota(jnp.int32, (block, block), 0)
    r_j = lax.broadcasted_iota(jnp.int32, (block, block), 1)
    t_i, t_j = r_i >> bits, r_j >> bits
    same_place = (r_i & (share // pieces - 1)) == (r_j & (share // pieces - 1))

    def pass_tokens(c, h):
        await_tokens(c, h, 2)
        give_tokens(c, h, 2, 1, token_mate(1))

    saves = []
    for i, (c, h) in enumerate(units):
        for d in hops:
            await_deal(c, h, d)
            if i + 1 < len(units):
                deal(*units[i + 1], d)
        allowed = same_place & (t_j <= t_i) & ((t_j >= starts[c]) | (t_j == t_i))
        mask = jnp.where(allowed, 1.0, 0.0)
        y = attention(xin[c, h].reshape(block, width), gain, w_q, w_o, mask)
        each = share // pieces
        latents[c, :, pl.ds(h * each, each), :] = y.reshape(n, each, width)
        tok[c, 0, pl.ds(h * block, block), :] = y * lax.rsqrt(jnp.sum(y * y, -1, keepdims=True) + EPSILON)
        give_tokens(c, h, 0, 2, token_mate(2))
        give_tokens(c, h, 0, 1, token_mate(1))
        if i >= 2:
            pass_tokens(*units[i - 2])
        if h == pieces - 1:
            saves.append(pltpu.make_async_copy(latents.at[c], latents_out.at[c], lat_sem.at[c]))
            saves[-1].start()
        across(i)
    pass_codes(early)
    ready(0, 0)
    await_codes(1, early + late)
    score(0, 0, 0)
    score(0, 0, 1)
    ready(1, 0)
    score(1, 0, 0)
    score(1, 0, 1)
    for i in range(len(units) - 2, len(units)):
        if units[i][0] == 0:
            pass_tokens(*units[i])
    pass_codes(late)
    evens = range(2, blocks, 2)
    odds = range(3, blocks, 2)
    for r in evens:
        score(0, 0, r)
        score(1, 0, r)
    ready(0, 1)
    for r in (0, 1, *evens):
        score(0, 1, r)
    for i in range(len(units) - 2, len(units)):
        if units[i][0]:
            pass_tokens(*units[i])
    for r in odds:
        await_codes(r, early + late)
        score(0, 0, r)
        score(0, 1, r)
    share_totals(0)
    for r in odds:
        score(1, 0, r)
    ready(1, 1)
    for r in range(blocks):
        score(1, 1, r)
    share_totals(1)
    ones = jnp.ones((8, lanes), BF16)

    def term(c, r, h, inv):
        first, size = spans[h]
        p = weights[c, r, pl.ds(first, size), :] * inv
        at = pl.ds(c * tokens, tokens)
        sums = dot(p.astype(BF16), unit[at, :])
        k = p[:, :lanes]
        for i in range(1, tokens // lanes):
            k = k + p[:, i * lanes : (i + 1) * lanes]
        at = pl.ds(first, size)
        if c:
            sums = part_sums[r, at, :] + sums
            k = counted[r, at, :] + k
        part_sums[r, at, :] = sums
        counted[r, at, :] = k
        if c == clips - 1 and first + size == rows:
            kh, kl = split(counted[r])
            cnt = dot(ones, kh, NT) + dot(ones, kl, NT)
            if rows < width:
                cnt = jnp.concatenate([cnt, jnp.zeros((8, width - rows), F32)], 1)
            part_sums[r, pl.ds(rows, 8), :] = cnt

    def route(h):
        bits = list(range(stages))
        return bits[1::-1] + bits[2:] if h < swapped else bits

    def stage_of(r, h):
        k = 0
        while k < stages and not (r >> route(h)[k]) & 1:
            k += 1
        return k

    def slot(r, k, h):
        cleared = [sum(1 << j for j in route(h)[: i + 1]) for i in range(stages)]
        places_at = [(i, q) for i in range(stages) for q in range(blocks) if not q & cleared[i]]
        return places_at.index((k, r))

    inv = {}
    made = set()

    def make(r, h, c):
        if (r, h, c) not in made:
            made.add((r, h, c))
            if h == parts - 1 and c == clips - 1:
                for g in range(h):
                    make(r, g, c)
            for b in range(c):
                make(r, h, b)
            if c not in inv:
                inv[c] = inverse_totals(c)
            term(c, r, h, inv[c])

    jobs = [(r, h) for r in range(blocks) for h in range(parts)]
    jobs.sort(key=lambda job: (stage_of(*job), -(job[1] < swapped) if stage_of(*job) == 0 else job[1] < swapped, -job[0], job[1]))
    for r, h in jobs[: 2 * parts]:
        make(r, h, 0)
    for r, h in jobs:
        make(r, h, clips - 1)
        k = stage_of(r, h)
        first, size = spans[h]
        at = pl.ds(first, size + (8 if h == parts - 1 else 0))
        for j in range(k):
            i = slot(r, j, h)
            remote(arrived.at[i, at], arrived.at[i, at], r_send.at[i, h], r_recv.at[i, h], me).wait_recv()
            part_sums[r, at, :] = part_sums[r, at, :] + arrived[i, at, :]
        if r:
            j = route(h)[k]
            i = slot(r ^ (1 << j), k, h)
            send(part_sums.at[r, at], arrived.at[i, at], r_send.at[i, h], r_recv.at[i, h], block_mate(1 << j))
        else:
            saves.append(pltpu.make_async_copy(part_sums.at[r, at], terms_out.at[at], out_sem.at[h]))
            saves[-1].start()
    for cp in pending:
        cp.wait_send()
    for cp in saves:
        cp.wait()


def finish(found, terms, code_sums, code_counts, latents, new_sums, new_counts, new_codebook):
    rows, width = code_sums.shape
    latents[...] = found[...]
    sums = DECAY_RATE * code_sums[...] + (1.0 - DECAY_RATE) * terms[:rows, :]
    counts = DECAY_RATE * code_counts[...] + (1.0 - DECAY_RATE) * terms[rows : rows + 1, :rows]
    new_sums[...] = sums
    new_counts[...] = counts
    new_codebook[...] = sums / jnp.transpose(jnp.broadcast_to(counts, (width, rows)))


def local(n, video, clip_start, gain_space, qkv_space, out_space, gain_time, qkv_time, out_time, code_sums, code_counts):
    clips, _, places, width = video.shape
    rows = code_sums.shape[0]
    share, blocks, mates = places // n, n // 4, 4
    sizes = [32, 32] + [64] * (rows // 64 - 1)
    spans = [(sum(sizes[:i]), z) for i, z in enumerate(sizes)]
    parts = len(spans)
    pieces = 1
    tokens = mates * places
    vmem = pl.BlockSpec(memory_space=pltpu.VMEM)
    hbm = pl.BlockSpec(memory_space=pl.ANY)
    dma = pltpu.SemaphoreType.DMA
    found, terms = pl.pallas_call(
        functools.partial(body, n, spans),
        out_shape=(
            jax.ShapeDtypeStruct((clips, n, share, width), F32),
            jax.ShapeDtypeStruct((rows + 8, width), F32),
        ),
        in_specs=[hbm, pl.BlockSpec(memory_space=pltpu.SMEM), vmem, hbm, hbm, vmem, hbm, hbm, hbm, vmem],
        out_specs=(hbm,) * 2,
        scratch_shapes=[
            pltpu.VMEM((clips, places, width), F32),
            pltpu.VMEM((width, 3 * width), F32),
            pltpu.VMEM((width, width), F32),
            pltpu.VMEM((width, 3 * width), F32),
            pltpu.VMEM((width, width), F32),
            pltpu.VMEM((rows, width), F32),
            pltpu.VMEM((clips, n, share, width), F32),
            dma((7,)), dma((clips,)), dma((parts,)),
            pltpu.VMEM((clips, places, width), F32),
            pltpu.VMEM((clips, pieces, n, share // pieces, width), F32),
            pltpu.VMEM((blocks, rows, width), F32),
            pltpu.VMEM((clips, mates, places, width), F32),
            pltpu.VMEM((clips, blocks, rows, tokens), F32),
            pltpu.VMEM((clips * tokens, width), BF16),
            pltpu.VMEM((2, clips * tokens, width), BF16),
            pltpu.VMEM((clips, 8, tokens), F32),
            pltpu.VMEM((clips, mates, 1, tokens), F32),
            pltpu.VMEM((blocks, rows, 128), F32),
            pltpu.VMEM((blocks, rows + 8, width), F32),
            pltpu.VMEM((blocks, rows + 8, width), F32),
            dma((clips, pieces, n)), dma((clips, pieces, n)),
            dma((blocks, 4)), dma((blocks, 4)),
            dma((clips, pieces, mates)), dma((clips, pieces, mates)),
            dma((clips, mates)), dma((clips, mates)),
            dma((blocks, parts)), dma((blocks, parts)),
        ],
        compiler_params=pltpu.CompilerParams(
            collective_id=0, has_side_effects=True, vmem_limit_bytes=60 * 2**20
        ),
        name="tokenizer",
    )(
        video.reshape(clips, places, width), clip_start, gain_space.reshape(1, -1), qkv_space, out_space,
        gain_time.reshape(1, -1), qkv_time, out_time, code_sums, code_counts.reshape(1, -1),
    )
    lat, sums, counts, book = pl.pallas_call(
        finish,
        out_shape=(
            jax.ShapeDtypeStruct((clips, n, share, width), F32),
            jax.ShapeDtypeStruct((rows, width), F32),
            jax.ShapeDtypeStruct((1, rows), F32),
            jax.ShapeDtypeStruct((rows, width), F32),
        ),
        in_specs=[vmem] * 4,
        out_specs=(vmem,) * 4,
        name="finish",
    )(found, terms, code_sums, code_counts.reshape(1, -1))
    return lat, sums, counts.reshape(rows), book


def solution(mesh):
    in_specs = (
        P("groups", "frames", None, None),
        P("groups"),
        P(),
        P(),
        P(),
        P(),
        P(),
        P(),
        P(("groups", "frames"), None),
        P(("groups", "frames")),
    )
    out_specs = (
        P("groups", None, "frames", None),
        P(("groups", "frames"), None),
        P(("groups", "frames")),
        P(("groups", "frames"), None),
    )
    fn = functools.partial(local, mesh.shape["frames"])
    return jax.shard_map(fn, mesh=mesh, in_specs=in_specs, out_specs=out_specs, check_vma=False)
```

```python
import functools

import jax
import jax.numpy as jnp
from jax import lax
from jax.experimental import pallas as pl
from jax.experimental.pallas import tpu as pltpu
from jax.sharding import PartitionSpec as P

HEADS = 4
ATTN_SCALE = 10.0
SOFTMAX_WARMTH = 0.05
DECAY_RATE = 0.9
EPSILON = 1e-06
F32 = jnp.float32
BF16 = jnp.bfloat16
NN = (((1,), (0,)), ((), ()))
NT = (((1,), (1,)), ((), ()))


def split(a):
    hi = a.astype(BF16)
    return hi, (a - hi.astype(F32)).astype(BF16)


def dot(a, b, dims=NN):
    return lax.dot_general(a, b, dims, preferred_element_type=F32)


def dot3(a, b, dims=NN):
    return dot(a[0], b[0], dims) + (dot(a[0], b[1], dims) + dot(a[1], b[0], dims))


def dot2(a, b, dims=NN):
    return dot(a[0], b, dims) + dot(a[1], b, dims)


def attention(x, gain, w_qkv, w_out, mask, between=None):
    rows, width = x.shape
    hd = width // HEADS
    pair = 2 * hd
    lane_i = lax.broadcasted_iota(jnp.int32, (width, width), 0) // hd
    lane_j = lax.broadcasted_iota(jnp.int32, (width, width), 1) // hd
    same_head = jnp.where(lane_i == lane_j, 1.0, 0.0).astype(BF16)
    first = lax.broadcasted_iota(jnp.int32, (rows, pair), 1) < hd

    def product(a, w):
        ah, al = split(a)
        both = dot(jnp.concatenate([ah, al], 0), w[0])
        return both[:rows] + (both[rows:] + dot(ah, w[1]))

    normed = x * lax.rsqrt(jnp.mean(x * x, -1, keepdims=True) + EPSILON) * gain
    packed = product(normed, w_qkv)
    q, k, v = packed[:, :width], packed[:, width : 2 * width], packed[:, 2 * width :]
    squares = dot(jnp.concatenate(split(q * q) + split(k * k), 0), same_head)
    q = q * lax.rsqrt(squares[:rows] + squares[rows : 2 * rows] + EPSILON) * ATTN_SCALE
    k = k * lax.rsqrt(squares[2 * rows : 3 * rows] + squares[3 * rows :] + EPSILON)
    if between is not None:
        between()
    mixed = []
    for p in range(HEADS // 2):
        at = slice(p * pair, (p + 1) * pair)
        qh = q[:, at].astype(BF16).astype(F32)
        kh = k[:, at].astype(BF16).astype(F32)
        ql = pltpu.roll(q[:, at] - qh, hd, 1)
        kr = pltpu.roll(kh, hd, 1)
        kl = k[:, at] - kh
        s_a = dot(
            jnp.concatenate([jnp.where(first, qh, ql), jnp.where(first, qh, 0.0)], 1).astype(BF16),
            jnp.concatenate([jnp.where(first, kh, kr), kl], 1).astype(BF16), NT,
        )
        s_b = dot(
            jnp.concatenate([jnp.where(first, ql, qh), jnp.where(first, 0.0, qh)], 1).astype(BF16),
            jnp.concatenate([jnp.where(first, kr, kh), kl], 1).astype(BF16), NT,
        )
        e_a, e_b = jnp.exp(s_a), jnp.exp(s_b)
        if mask is not None:
            e_a, e_b = e_a * mask, e_b * mask
        e = jnp.concatenate([e_a, e_b], 0)
        eh, el = split(e)
        vh, vl = split(v[:, at])
        o = dot(eh, jnp.concatenate([vh, vl], 1))
        o = o[:, :pair] + (o[:, pair:] + dot(el, vh))
        o = o / jnp.sum(e, -1, keepdims=True)
        mixed.append(jnp.where(first, o[:rows], o[rows:]))
    return x + product(jnp.concatenate(mixed, 1), w_out)


def body(
    n,
    spans,
    video_in,
    starts,
    gain_space,
    qkv_space_in,
    out_space_in,
    gain_time,
    qkv_time_in,
    out_time_in,
    code_sums_in,
    code_counts,
    latents_out,
    terms_out,
    video,
    qkv_space,
    out_space,
    qkv_time,
    out_time,
    code_sums,
    latents,
    in_sem,
    lat_sem,
    out_sem,
    spaced,
    xin,
    codes,
    tok,
    weights,
    unit,
    warm,
    total,
    den,
    counted,
    part_sums,
    arrived,
    a2a_send,
    a2a_recv,
    g_send,
    g_recv,
    t_send,
    t_recv,
    d_send,
    d_recv,
    r_send,
    r_recv,
):
    clips, places, width = video.shape
    share = places // n
    pieces = xin.shape[1]
    rows = code_sums.shape[0]
    blocks = codes.shape[0]
    mates = tok.shape[1]
    stages = blocks.bit_length() - 1
    tokens = mates * places
    chunk, lanes = rows // 4, 128
    parts, swapped = len(spans), 1 if stages > 1 else 0
    code_bits = [1] + list(range(3, n.bit_length() - 1))

    me = lax.axis_index("frames")
    pending = []

    def flip(k):
        return (1 - 2 * ((me // 2**k) % 2)) * 2**k

    def token_mate(k):
        return me + (k & 1) * flip(0) + (k >> 1) * flip(2)

    def block_mate(r):
        to = me
        for j in range(stages):
            if (r >> j) & 1:
                to = to + flip(code_bits[j])
        return to

    def remote(src, dst, ssem, rsem, dev):
        return pltpu.make_async_remote_copy(
            src_ref=src, dst_ref=dst, send_sem=ssem, recv_sem=rsem,
            device_id={"frames": dev}, device_id_type=pl.DeviceIdType.MESH,
        )

    def send(src, dst, ssem, rsem, dev):
        cp = remote(src, dst, ssem, rsem, dev)
        cp.start()
        pending.append(cp)

    barrier = pltpu.get_barrier_semaphore()

    def greet(i, c):
        pl.semaphore_signal(
            barrier, inc=1, device_id={"frames": lax.rem(me + i, n)},
            device_id_type=pl.DeviceIdType.MESH,
        )
        return c

    lax.fori_loop(1, n, greet, 0)
    loads = {}
    for i, (name, src, dst) in enumerate((
        ("video0", video_in.at[0], video.at[0]), ("qkv_space", qkv_space_in, qkv_space),
        ("out_space", out_space_in, out_space), ("code_sums", code_sums_in, code_sums),
        ("video1", video_in.at[pl.ds(1, clips - 1)], video.at[pl.ds(1, clips - 1)]),
        ("qkv_time", qkv_time_in, qkv_time), ("out_time", out_time_in, out_time),
    )):
        loads[name] = pltpu.make_async_copy(src, dst, in_sem.at[i])
        loads[name].start()

    def code_copy(r, q, ch, dev):
        at = pl.ds(ch * chunk, chunk)
        return remote(codes.at[r, at], codes.at[q, at], g_send.at[q, ch], g_recv.at[q, ch], dev)

    def give_codes(r, j, ch):
        cp = code_copy(r, r ^ (1 << j), ch, block_mate(1 << j))
        cp.start()
        pending.append(cp)

    def await_codes(r, chs):
        for ch in chs:
            code_copy(r, r, ch, me).wait_recv()

    def pass_codes(chs):
        for j in range(1, stages):
            for r in range(1 << j, 2 << j, 2):
                for ch in chs:
                    await_codes(r, [ch])
                    for i in range(j + 1, stages):
                        give_codes(r, i, ch)
                    give_codes(r, 0, ch)

    def token_copy(c, h, q, p, dev):
        at = pl.ds(h * (places // pieces), places // pieces)
        return remote(tok.at[c, q, at], tok.at[c, p, at], t_send.at[c, h, p], t_recv.at[c, h, p], dev)

    def give_tokens(c, h, q, k, dev):
        cp = token_copy(c, h, q, q ^ k, dev)
        cp.start()
        pending.append(cp)

    def await_tokens(c, h, q):
        token_copy(c, h, q, q, me).wait_recv()

    code_at = [-1, -1, 0, 0]
    early = [ch for ch in range(4) if code_at[ch] < 0]
    late = [ch for ch in range(4) if code_at[ch] >= 0]

    def across(when):
        for ch in range(4 if when == -2 else 0):
            give_codes(0, 0, ch)
        for ch in range(4):
            if code_at[ch] == when:
                for j in range(1, stages):
                    give_codes(0, j, ch)

    def enter():
        loads["code_sums"].wait()
        own = code_sums[...] / jnp.transpose(jnp.broadcast_to(code_counts[...], (width, rows)))
        codes[0] = own * lax.rsqrt(jnp.sum(own * own, -1, keepdims=True) + EPSILON)
        pl.semaphore_wait(barrier, n - 1)
        across(-2)

    loads["qkv_space"].wait()
    loads["out_space"].wait()
    w_q, w_o = split(qkv_space[...]), split(out_space[...])
    gain = gain_space[...]
    hops = sorted(range(1, n), key=lambda d: abs(2 * d - n))

    def deal(c, h, d):
        to = lax.rem(me + d, n)
        send(
            spaced.at[c, pl.ds(pl.multiple_of(to * share + h * places // n // pieces, 8), share // pieces), :],
            xin.at[c, h, me], a2a_send.at[c, h, d], a2a_recv.at[c, h, d], to,
        )

    def await_deal(c, h, d):
        src = lax.rem(me + n - d, n)
        remote(xin.at[c, h, src], xin.at[c, h, src], a2a_send.at[c, h, d], a2a_recv.at[c, h, d], me).wait_recv()

    def keep(c):
        for h in range(pieces):
            at = pl.ds(pl.multiple_of(me * share + h * places // n // pieces, 8), share // pieces)
            xin[c, h, me] = spaced[c, at, :]

    units = [(c, h) for c in range(clips) for h in range(pieces)]
    for c in range(clips):
        if c < 2:
            loads["video%d" % c].wait()
        spaced[c] = attention(video[c], gain, w_q, w_o, None, enter if c == 0 else None)
        if c < 1:
            for d in hops:
                deal(*units[c], d)
        keep(c)
    across(-1)
    loads["qkv_time"].wait()
    loads["out_time"].wait()

    def ready(c, h, quarters=(0, 1)):
        for q in (2 * h + i for i in quarters):
            if q % 2:
                for i in range(pieces):
                    await_tokens(c, i, q)
            u = tok[c, q]
            at = pl.ds((c * mates + q) * places, places)
            unit[at, :] = u.astype(BF16)
            warm[0, at, :], warm[1, at, :] = split(u * (1.0 / SOFTMAX_WARMTH))

    def score(c, h, r, quarter=None):
        two = 2 * places if quarter is None else places
        begin = 2 * h * places + (quarter or 0) * places
        at = pl.ds(c * tokens + begin, two)
        e = jnp.exp(dot3(split(codes[r]), (warm[0, at, :], warm[1, at, :]), NT))
        at = pl.ds(begin, two)
        weights[c, r, :, at] = e
        t = jnp.sum(e.reshape(rows // 8, 8, two), 0)
        total[c, :, at] = t if r == 0 else total[c, :, at] + t

    def share_totals(c):
        den[c, 0] = jnp.sum(total[c], 0, keepdims=True)
        for k in range(1, mates):
            send(den.at[c, 0], den.at[c, k], d_send.at[c, k], d_recv.at[c, k], token_mate(k))

    def inverse_totals(c):
        for k in range(1, mates):
            remote(den.at[c, k], den.at[c, k], d_send.at[c, k], d_recv.at[c, k], me).wait_recv()
        full = [
            sum(den[c, k, :, pl.ds((q ^ k) * places, places)] for k in range(mates)) for q in range(mates)
        ]
        return 1.0 / jnp.concatenate(full, 1)

    w_q, w_o = split(qkv_time[...]), split(out_time[...])
    gain = gain_time[...]
    block = places // pieces
    bits = (share // pieces).bit_length() - 1
    r_i = lax.broadcasted_iota(jnp.int32, (block, block), 0)
    r_j = lax.broadcasted_iota(jnp.int32, (block, block), 1)
    t_i, t_j = r_i >> bits, r_j >> bits
    same_place = (r_i & (share // pieces - 1)) == (r_j & (share // pieces - 1))

    def pass_tokens(c, h):
        await_tokens(c, h, 2)
        give_tokens(c, h, 2, 1, token_mate(1))

    saves = []
    for i, (c, h) in enumerate(units):
        for d in hops:
            await_deal(c, h, d)
            if i + 1 < len(units):
                deal(*units[i + 1], d)
        allowed = same_place & (t_j <= t_i) & ((t_j >= starts[c]) | (t_j == t_i))
        mask = jnp.where(allowed, 1.0, 0.0)
        y = attention(xin[c, h].reshape(block, width), gain, w_q, w_o, mask)
        each = share // pieces
        latents[c, :, pl.ds(h * each, each), :] = y.reshape(n, each, width)
        tok[c, 0, pl.ds(h * block, block), :] = y * lax.rsqrt(jnp.sum(y * y, -1, keepdims=True) + EPSILON)
        give_tokens(c, h, 0, 2, token_mate(2))
        give_tokens(c, h, 0, 1, token_mate(1))
        if i >= 2:
            pass_tokens(*units[i - 2])
        if h == pieces - 1:
            saves.append(pltpu.make_async_copy(latents.at[c], latents_out.at[c], lat_sem.at[c]))
            saves[-1].start()
        across(i)
    pass_codes(early)
    ready(0, 0)
    await_codes(1, early + late)
    score(0, 0, 0)
    score(0, 0, 1)
    ready(1, 0)
    score(1, 0, 0)
    score(1, 0, 1)
    for i in range(len(units) - 2, len(units)):
        if units[i][0] == 0:
            pass_tokens(*units[i])
    pass_codes(late)
    evens = range(2, blocks, 2)
    odds = range(3, blocks, 2)
    for r in evens:
        score(0, 0, r)
        score(1, 0, r)
    ready(0, 1)
    for r in (0, 1, *evens):
        score(0, 1, r)
    for i in range(len(units) - 2, len(units)):
        if units[i][0]:
            pass_tokens(*units[i])
    for r in odds:
        await_codes(r, early + late)
        score(0, 0, r)
        score(0, 1, r)
    share_totals(0)
    for r in odds:
        score(1, 0, r)
    for quarter in range(2):
        ready(1, 1, (quarter,))
        for r in range(blocks):
            score(1, 1, r, quarter)
    share_totals(1)
    ones = jnp.ones((8, lanes), BF16)

    def term(c, r, h, inv):
        first, size = spans[h]
        p = weights[c, r, pl.ds(first, size), :] * inv
        at = pl.ds(c * tokens, tokens)
        sums = dot(p.astype(BF16), unit[at, :])
        k = p[:, :lanes]
        for i in range(1, tokens // lanes):
            k = k + p[:, i * lanes : (i + 1) * lanes]
        at = pl.ds(first, size)
        if c:
            sums = part_sums[r, at, :] + sums
            k = counted[r, at, :] + k
        part_sums[r, at, :] = sums
        counted[r, at, :] = k
        if c == clips - 1 and first + size == rows:
            kh, kl = split(counted[r])
            cnt = dot(ones, kh, NT) + dot(ones, kl, NT)
            if rows < width:
                cnt = jnp.concatenate([cnt, jnp.zeros((8, width - rows), F32)], 1)
            part_sums[r, pl.ds(rows, 8), :] = cnt

    def route(h):
        bits = list(range(stages))
        return bits[1::-1] + bits[2:] if h < swapped else bits

    def stage_of(r, h):
        k = 0
        while k < stages and not (r >> route(h)[k]) & 1:
            k += 1
        return k

    def slot(r, k, h):
        cleared = [sum(1 << j for j in route(h)[: i + 1]) for i in range(stages)]
        places_at = [(i, q) for i in range(stages) for q in range(blocks) if not q & cleared[i]]
        return places_at.index((k, r))

    inv = {}
    made = set()

    def make(r, h, c):
        if (r, h, c) not in made:
            made.add((r, h, c))
            if h == parts - 1 and c == clips - 1:
                for g in range(h):
                    make(r, g, c)
            for b in range(c):
                make(r, h, b)
            if c not in inv:
                inv[c] = inverse_totals(c)
            term(c, r, h, inv[c])

    jobs = [(r, h) for r in range(blocks) for h in range(parts)]
    jobs.sort(key=lambda job: (stage_of(*job), -(job[1] < swapped) if stage_of(*job) == 0 else job[1] < swapped, -job[0], job[1]))
    for r, h in jobs[: 2 * parts]:
        make(r, h, 0)
    for r, h in jobs:
        make(r, h, clips - 1)
        k = stage_of(r, h)
        first, size = spans[h]
        at = pl.ds(first, size + (8 if h == parts - 1 else 0))
        for j in range(k):
            i = slot(r, j, h)
            remote(arrived.at[i, at], arrived.at[i, at], r_send.at[i, h], r_recv.at[i, h], me).wait_recv()
            part_sums[r, at, :] = part_sums[r, at, :] + arrived[i, at, :]
        if r:
            j = route(h)[k]
            i = slot(r ^ (1 << j), k, h)
            send(part_sums.at[r, at], arrived.at[i, at], r_send.at[i, h], r_recv.at[i, h], block_mate(1 << j))
        else:
            saves.append(pltpu.make_async_copy(part_sums.at[r, at], terms_out.at[at], out_sem.at[h]))
            saves[-1].start()
    for cp in pending:
        cp.wait_send()
    for cp in saves:
        cp.wait()


def finish(found, terms, code_sums, code_counts, latents, new_sums, new_counts, new_codebook):
    rows, width = code_sums.shape
    latents[...] = found[...]
    sums = DECAY_RATE * code_sums[...] + (1.0 - DECAY_RATE) * terms[:rows, :]
    counts = DECAY_RATE * code_counts[...] + (1.0 - DECAY_RATE) * terms[rows : rows + 1, :rows]
    new_sums[...] = sums
    new_counts[...] = counts
    new_codebook[...] = sums / jnp.transpose(jnp.broadcast_to(counts, (width, rows)))


def local(n, video, clip_start, gain_space, qkv_space, out_space, gain_time, qkv_time, out_time, code_sums, code_counts):
    clips, _, places, width = video.shape
    rows = code_sums.shape[0]
    share, blocks, mates = places // n, n // 4, 4
    sizes = [32, 32] + [64] * (rows // 64 - 1)
    spans = [(sum(sizes[:i]), z) for i, z in enumerate(sizes)]
    parts = len(spans)
    pieces = 1
    tokens = mates * places
    vmem = pl.BlockSpec(memory_space=pltpu.VMEM)
    hbm = pl.BlockSpec(memory_space=pl.ANY)
    dma = pltpu.SemaphoreType.DMA
    found, terms = pl.pallas_call(
        functools.partial(body, n, spans),
        out_shape=(
            jax.ShapeDtypeStruct((clips, n, share, width), F32),
            jax.ShapeDtypeStruct((rows + 8, width), F32),
        ),
        in_specs=[hbm, pl.BlockSpec(memory_space=pltpu.SMEM), vmem, hbm, hbm, vmem, hbm, hbm, hbm, vmem],
        out_specs=(hbm,) * 2,
        scratch_shapes=[
            pltpu.VMEM((clips, places, width), F32),
            pltpu.VMEM((width, 3 * width), F32),
            pltpu.VMEM((width, width), F32),
            pltpu.VMEM((width, 3 * width), F32),
            pltpu.VMEM((width, width), F32),
            pltpu.VMEM((rows, width), F32),
            pltpu.VMEM((clips, n, share, width), F32),
            dma((7,)), dma((clips,)), dma((parts,)),
            pltpu.VMEM((clips, places, width), F32),
            pltpu.VMEM((clips, pieces, n, share // pieces, width), F32),
            pltpu.VMEM((blocks, rows, width), F32),
            pltpu.VMEM((clips, mates, places, width), F32),
            pltpu.VMEM((clips, blocks, rows, tokens), F32),
            pltpu.VMEM((clips * tokens, width), BF16),
            pltpu.VMEM((2, clips * tokens, width), BF16),
            pltpu.VMEM((clips, 8, tokens), F32),
            pltpu.VMEM((clips, mates, 1, tokens), F32),
            pltpu.VMEM((blocks, rows, 128), F32),
            pltpu.VMEM((blocks, rows + 8, width), F32),
            pltpu.VMEM((blocks, rows + 8, width), F32),
            dma((clips, pieces, n)), dma((clips, pieces, n)),
            dma((blocks, 4)), dma((blocks, 4)),
            dma((clips, pieces, mates)), dma((clips, pieces, mates)),
            dma((clips, mates)), dma((clips, mates)),
            dma((blocks, parts)), dma((blocks, parts)),
        ],
        compiler_params=pltpu.CompilerParams(
            collective_id=0, has_side_effects=True, vmem_limit_bytes=60 * 2**20
        ),
        name="tokenizer",
    )(
        video.reshape(clips, places, width), clip_start, gain_space.reshape(1, -1), qkv_space, out_space,
        gain_time.reshape(1, -1), qkv_time, out_time, code_sums, code_counts.reshape(1, -1),
    )
    lat, sums, counts, book = pl.pallas_call(
        finish,
        out_shape=(
            jax.ShapeDtypeStruct((clips, n, share, width), F32),
            jax.ShapeDtypeStruct((rows, width), F32),
            jax.ShapeDtypeStruct((1, rows), F32),
            jax.ShapeDtypeStruct((rows, width), F32),
        ),
        in_specs=[vmem] * 4,
        out_specs=(vmem,) * 4,
        name="finish",
    )(found, terms, code_sums, code_counts.reshape(1, -1))
    return lat, sums, counts.reshape(rows), book


def solution(mesh):
    in_specs = (
        P("groups", "frames", None, None),
        P("groups"),
        P(),
        P(),
        P(),
        P(),
        P(),
        P(),
        P(("groups", "frames"), None),
        P(("groups", "frames")),
    )
    out_specs = (
        P("groups", None, "frames", None),
        P(("groups", "frames"), None),
        P(("groups", "frames")),
        P(("groups", "frames"), None),
    )
    fn = functools.partial(local, mesh.shape["frames"])
    return jax.shard_map(fn, mesh=mesh, in_specs=in_specs, out_specs=out_specs, check_vma=False)
```
